32 devices in a mesh: seq: 8 (over y, x, core), head: 4 (over z).
Axes of the slice: x: 2, y: 2, z: 4, core: 2. Of those that a mesh axis runs over, the one named last changes fastest.
Arguments:
- hidden: bfloat16 [2, 2048, 768], P(None, 'seq'), may hold values from -6 to 6
- cotangent: bfloat16 [2, 2048, 768], P(None, 'seq'), may hold values from -6 to 6
- norm_gain: float32 [2, 768], replicated, may hold values from 0.5 to 1.5
- w_in_zx: bfloat16 [2, 768, 2, 1536], P(None, None, None, 'head'), may hold values from -0.21875 to 0.21875
- w_in_dt: bfloat16 [2, 768, 24], P(None, None, 'head'), may hold values from -0.21875 to 0.21875
- w_in_bc: bfloat16 [2, 768, 256], replicated, may hold values from -0.21875 to 0.21875
- conv_x: float32 [2, 4, 1536], P(None, None, 'head'), may hold values from -3 to 3
- conv_x_bias: float32 [2, 1536], P(None, 'head'), may hold values from -3 to 3
- conv_bc: float32 [2, 4, 256], replicated, may hold values from -3 to 3
- conv_bc_bias: float32 [2, 256], replicated, may hold values from -3 to 3
- dt_bias: float32 [2, 24], P(None, 'head'), may hold values from -10 to -4
- a_log: float32 [2, 24], P(None, 'head'), may hold values from 0 to 2.77
- d_skip: float32 [2, 24], P(None, 'head'), may hold values from 0.5 to 1.5
- gate_norm: float32 [2, 1536], P(None, 'head'), may hold values from 0.5 to 1.5
- w_out: bfloat16 [2, 1536, 768], P(None, 'head'), may hold values from -0.15625 to 0.15625
Outputs:
- final_out: float32 [2, 2048, 768], P(None, 'seq')
- hidden_grad: float32 [2, 2048, 768], P(None, 'seq')
- norm_gain_grad: float32 [2, 768], replicated
- w_in_zx_grad: float32 [2, 768, 2, 1536], P(None, None, None, 'head')
- w_in_dt_grad: float32 [2, 768, 24], P(None, None, 'head')
- w_in_bc_grad: float32 [2, 768, 256], replicated
- conv_x_grad: float32 [2, 4, 1536], P(None, None, 'head')
- conv_x_bias_grad: float32 [2, 1536], P(None, 'head')
- conv_bc_grad: float32 [2, 4, 256], replicated
- conv_bc_bias_grad: float32 [2, 256], replicated
- dt_bias_grad: float32 [2, 24], P(None, 'head')
- a_log_grad: float32 [2, 24], P(None, 'head')
- d_skip_grad: float32 [2, 24], P(None, 'head')
- gate_norm_grad: float32 [2, 1536], P(None, 'head')
- w_out_grad: float32 [2, 1536, 768], P(None, 'head')
The draws below stay inside these ranges and needn't reach their ends.
All inputs are finite; a program needn't handle non-finite values.
Results may differ from the reference program's by a relative error of at most 0.015.
Values may be sent and summed in bfloat16 or wider, within the bound.
No kernel may reach another device: no remote copies, remote signals or barrier semaphores. Data moves between devices by JAX's collectives and lax.ppermute only.
A program may use at most 128 MiB of HBM per device.

```python
import jax
import jax.numpy as jnp
from jax import lax

D = 768
HEADS = 24
HEADDIM = 64
STATE = 128
CONV = 4
LAYERS = 2
SEQS = 2
INNER = 1536
SPAN = 256
SEQLEN = 2048


def draw_dt_bias(key, part):
    return jax.random.uniform(key, (LAYERS, HEADS), jnp.float32, -9.0, -4.0)


def draw_a_log(key, part):
    return jax.random.uniform(key, (LAYERS, HEADS), jnp.float32, 0.0, 2.77)


def levels(own_key, extent, shards, least, high):
    level, own = 1.0, jax.random.fold_in(own_key, 6)
    for dim, shards_of in shards:
        heights = jnp.exp(jax.random.uniform(jax.random.fold_in(own, dim), (shards_of,), jnp.float32, least / len(shards), high / len(shards)))
        level = level * jnp.repeat(heights, extent[dim] // shards_of).reshape([-1 if axis == dim else 1 for axis in range(len(extent))])
    return level


def gaussian(stream_key, shape, scale, reach, cuts=(), kind=jnp.bfloat16):
    values = scale * jax.random.normal(stream_key, shape, jnp.float32)
    if cuts:
        values = values * levels(stream_key, shape, cuts, -0.22, 0.18)
    return jnp.clip(values, -reach, reach).astype(kind)


def setup_inputs(seed: int = 0) -> dict:
    arg_keys = jax.random.split(jax.random.key(seed), 16)
    return {
        "hidden": gaussian(arg_keys[0], (SEQS, SEQLEN, D), 1.0, 6.0, ((1, 8),)),
        "cotangent": gaussian(arg_keys[1], (SEQS, SEQLEN, D), 1.0, 6.0, ((1, 8),)),
        "norm_gain": jnp.clip(1.0 + 0.1 * jax.random.normal(arg_keys[2], (LAYERS, D), jnp.float32), 0.5, 1.5),
        "w_in_zx": gaussian(arg_keys[3], (LAYERS, D, 2, INNER), D ** -0.5, 0.21875, ((3, 4),)),
        "w_in_dt": gaussian(arg_keys[4], (LAYERS, D, HEADS), D ** -0.5, 0.21875, ((2, 4),)),
        "w_in_bc": gaussian(arg_keys[5], (LAYERS, D, 2 * STATE), D ** -0.5, 0.21875),
        "conv_x": gaussian(arg_keys[6], (LAYERS, CONV, INNER), CONV ** -0.5, 3.0, ((2, 4),), jnp.float32),
        "conv_x_bias": gaussian(arg_keys[7], (LAYERS, INNER), 0.5, 3.0, ((1, 4),), jnp.float32),
        "conv_bc": gaussian(arg_keys[8], (LAYERS, CONV, 2 * STATE), CONV ** -0.5, 3.0, (), jnp.float32),
        "conv_bc_bias": gaussian(arg_keys[9], (LAYERS, 2 * STATE), 0.5, 3.0, (), jnp.float32),
        "dt_bias": draw_dt_bias(jax.random.fold_in(arg_keys[15], 71), 0),
        "a_log": draw_a_log(jax.random.fold_in(arg_keys[15], 71), 0),
        "d_skip": jnp.clip(0.5 + 1.0 * jax.random.uniform(arg_keys[12], (LAYERS, HEADS), jnp.float32) ** levels(arg_keys[12], (LAYERS, HEADS), ((1, 4),), -0.2, 0.2), 0.5, 1.5),
        "gate_norm": jnp.clip(1.0 + 0.1 * jax.random.normal(arg_keys[13], (LAYERS, INNER), jnp.float32), 0.5, 1.5),
        "w_out": gaussian(arg_keys[14], (LAYERS, INNER, D), INNER ** -0.5, 0.15625, ((1, 4),)),
    }


EPSILON = 1e-05
PRECISE = lax.Precision.HIGHEST

@jax.custom_vjp
def low(v):
    return lax.optimization_barrier(v.astype(jnp.bfloat16)).astype(jnp.float32)

@jax.custom_vjp
def low_back(v):
    return v

def low_keep(v):
    return (low(v), None)

def low_pass(kept, grad):
    return (grad,)

def back_keep(v):
    return (v, None)

def back_low(kept, grad):
    return (low(grad),)
low.defvjp(low_keep, low_pass)
low_back.defvjp(back_keep, back_low)

def causal_conv(values, kernel, offset):
    length = values.shape[1]
    tap_count = kernel.shape[0]
    padded = jnp.pad(values, ((0, 0), (tap_count - 1, 0), (0, 0)))
    result = offset + jnp.zeros_like(values)
    for tap_index in range(tap_count):
        result = result + kernel[tap_index] * padded[:, tap_index:tap_index + length]
    return result

def span_step(state_in, pieces):
    inputs, step_size, log_decay, b_rows, c_rows = pieces
    length = inputs.shape[1]
    cumulative = jnp.cumsum(log_decay, axis=1)
    places = jnp.arange(length)
    causal = (places[:, None] >= places[None, :])[None, :, :, None]
    spread = cumulative[:, :, None, :] - cumulative[:, None, :, :]
    decays = jnp.where(causal, jnp.exp(jnp.where(causal, spread, 0.0)), 0.0)
    scores = jnp.einsum('btn,bsn->bts', c_rows, b_rows, precision=PRECISE)
    mixing = scores[..., None] * decays * step_size[:, None, :, :]
    outputs = jnp.einsum('btsh,bshp->bthp', mixing, inputs, precision=PRECISE)
    outputs = outputs + jnp.exp(cumulative)[..., None] * jnp.einsum('btn,bhpn->bthp', c_rows, state_in, precision=PRECISE)
    final_sum = cumulative[:, -1]
    weights_tail = jnp.exp(final_sum[:, None, :] - cumulative) * step_size
    state_out = jnp.exp(final_sum)[:, :, None, None] * state_in + jnp.einsum('bsh,bshp,bsn->bhpn', weights_tail, inputs, b_rows, precision=PRECISE)
    return (state_out, outputs)

def scan_spans(inputs, step_size, log_decay, b_rows, c_rows):
    batch_count, length, head_count, head_size = inputs.shape
    block_count = length // SPAN

    def to_blocks(value):
        shaped = value.reshape((batch_count, block_count, SPAN) + value.shape[2:])
        return jnp.moveaxis(shaped, 1, 0)
    initial = jnp.zeros((batch_count, head_count, head_size, b_rows.shape[-1]), jnp.float32)
    unused, outputs = lax.scan(jax.checkpoint(span_step), initial, (to_blocks(inputs), to_blocks(step_size), to_blocks(log_decay), to_blocks(b_rows), to_blocks(c_rows)))
    return jnp.moveaxis(outputs, 0, 1).reshape(inputs.shape)

def mixer_layer(stream, gain, proj_zx, proj_dt, proj_bc, kernel_x, offset_x, kernel_bc, offset_bc, bias_dt, log_rate, skip_gain, gate_gain, proj_out):
    batch_count, length, width = stream.shape
    normed = low(stream * lax.rsqrt(lax.optimization_barrier(jnp.mean(stream * stream, -1, keepdims=True)) + EPSILON) * gain)
    projected = low_back(jnp.einsum('btd,dki->btki', normed, proj_zx, precision=PRECISE))
    gate_in = projected[:, :, 0]
    values_raw = low(projected[:, :, 1])
    states_raw = low(low_back(jnp.einsum('btd,dn->btn', normed, proj_bc, precision=PRECISE)))
    steps_raw = low_back(jnp.einsum('btd,dh->bth', normed, proj_dt, precision=PRECISE))
    values_conv = low(jax.nn.silu(causal_conv(values_raw, kernel_x, offset_x)))
    states_conv = low(jax.nn.silu(causal_conv(states_raw, kernel_bc, offset_bc)))
    step_size = jax.nn.softplus(steps_raw + bias_dt)
    log_decay = -jnp.exp(log_rate) * step_size
    inputs = values_conv.reshape(batch_count, length, HEADS, HEADDIM)
    mixed = scan_spans(inputs, step_size, log_decay, states_conv[..., :STATE], states_conv[..., STATE:]) + skip_gain[:, None] * inputs
    gated = mixed.reshape(batch_count, length, INNER) * jax.nn.silu(gate_in)
    normed_out = low(gated * lax.rsqrt(lax.optimization_barrier(jnp.mean(gated * gated, -1, keepdims=True)) + EPSILON) * gate_gain)
    branch = low_back(jnp.einsum('bti,id->btd', normed_out, proj_out, precision=PRECISE))
    return stream + branch

def reference(hidden, cotangent, norm_gain, w_in_zx, w_in_dt, w_in_bc, conv_x, conv_x_bias, conv_bc, conv_bc_bias, dt_bias, a_log, d_skip, gate_norm, w_out):
    weights = tuple((array_item.astype(jnp.float32) for array_item in (norm_gain, w_in_zx, w_in_dt, w_in_bc, conv_x, conv_x_bias, conv_bc, conv_bc_bias, dt_bias, a_log, d_skip, gate_norm, w_out)))

    def forward(stream, *params):
        for depth_index in range(LAYERS):
            stream = mixer_layer(stream, *[array_item[depth_index] for array_item in params])
        return stream
    final_out, pullback = jax.vjp(forward, hidden.astype(jnp.float32), *weights)
    gradients = pullback(cotangent.astype(jnp.float32))
    return (final_out, gradients[0], gradients[1], gradients[2], gradients[3], gradients[4], gradients[5], gradients[6], gradients[7], gradients[8], gradients[9], gradients[10], gradients[11], gradients[12], gradients[13])
```

```python
import jax
import jax.numpy as jnp
from jax import lax
from jax.experimental import pallas as pl
from jax.experimental.pallas import tpu as pltpu
from jax.sharding import PartitionSpec as P

EPSILON = 1e-05
PRECISE = lax.Precision.HIGHEST
LANES = 128
HALO = 16
F32 = jnp.float32
BF16 = jnp.bfloat16


def nn(a, b, precision=None):
    return lax.dot_general(
        a, b, (((1,), (0,)), ((), ())), precision=precision, preferred_element_type=F32
    )


def nt(a, b, precision=None):
    return lax.dot_general(
        a, b, (((1,), (1,)), ((), ())), precision=precision, preferred_element_type=F32
    )


def tn(a, b, precision=None):
    return lax.dot_general(
        a, b, (((0,), (0,)), ((), ())), precision=precision, preferred_element_type=F32
    )


def iota(shape, axis):
    return lax.broadcasted_iota(jnp.int32, shape, axis)


def sigmoid(v):
    return 1.0 / (1.0 + jnp.exp(-v))


def softplus(v):
    small = jnp.exp(-jnp.abs(v))
    grown = 1.0 + small
    gap = grown - 1.0
    log1p = jnp.where(gap == 0.0, small, jnp.log(grown) * small / jnp.where(gap == 0.0, 1.0, gap))
    return jnp.maximum(v, 0.0) + log1p


def spread_heads(inner, head_size):
    return (iota((LANES, inner), 1) // head_size == iota((LANES, inner), 0)).astype(F32)


def lower_tri(length):
    return (iota((length, length), 0) >= iota((length, length), 1)).astype(F32)


def call(kernel, outs, args, specs=None, scratch=(), prefetch=None):
    whole = lambda a: pl.BlockSpec(a.shape, lambda *_, n=a.ndim: (0,) * n)
    in_specs = [whole(a) if s is None else s for a, s in zip(args, specs or [None] * len(args))]
    out_shape = [jax.ShapeDtypeStruct(s, d) for s, d in outs]
    return pl.pallas_call(
        kernel,
        grid_spec=pltpu.PrefetchScalarGridSpec(
            num_scalar_prefetch=0 if prefetch is None else 1,
            grid=(1,),
            in_specs=in_specs,
            out_specs=[whole(o) for o in out_shape],
            scratch_shapes=list(scratch),
        ),
        out_shape=out_shape,
    )(*(() if prefetch is None else (prefetch,)), *args)


def layer_spec(array, layer, extra=None):
    shape = (None,) + array.shape[1:]
    index = (layer,) + (0,) * (array.ndim - 1)
    if extra is not None:
        shape = (None, None) + array.shape[2:]
        index = (layer, extra) + (0,) * (array.ndim - 2)
    return pl.BlockSpec(shape, lambda *_: index)


def forward_kernel(dims):
    batch, length, inner, heads, head_size, state = dims

    def kernel(
        normed, halo, w_gate, w_val, w_bc, w_dt, taps_x, taps_bc, head_par,
        gate_out, padx_out, padbc_out, prex_out, prebc_out, local_out, step_out, cum_out, pay_out,
        y_buf,
    ):
        spread = spread_heads(inner, head_size)
        tri = lower_tri(length)
        causal = iota((length, length), 0) >= iota((length, length), 1)
        rates = -jnp.exp(head_par[1:2])
        skip = nn(head_par[...], spread, PRECISE)[2:3]
        extra = jnp.zeros((1, LANES), F32)
        for b in range(batch):
            rows = slice(b * length, (b + 1) * length)
            x_in = normed[rows]
            x_halo = halo[b * HALO : (b + 1) * HALO]
            gate_out[rows] = nn(x_in, w_gate[...])
            acts = []
            for weight, taps, pad_out, pre_out in (
                (w_val, taps_x, padx_out, prex_out),
                (w_bc, taps_bc, padbc_out, prebc_out),
            ):
                base = b * (length + 8)
                pad_out[base : base + 8] = nn(x_halo, weight[...])[HALO - 8 :].astype(BF16).astype(F32)
                pad_out[base + 8 : base + 8 + length] = nn(x_in, weight[...]).astype(BF16).astype(F32)
                pre = taps[4:5] + taps[0:1] * pad_out[base + 5 : base + 5 + length]
                for k in range(1, 4):
                    pre = pre + taps[k : k + 1] * pad_out[base + 5 + k : base + 5 + k + length]
                pre_out[rows] = pre
                acts.append((pre * sigmoid(pre)).astype(BF16))
            x_act, bc = acts
            b_rows, c_rows = bc[:, :state], bc[:, state:]
            step_raw = nn(x_in, w_dt[...]) + head_par[0:1]
            step = softplus(step_raw)
            cum = nn(tri, rates * step, PRECISE)
            step_out[rows] = step_raw
            cum_out[rows] = cum
            total = cum[length - 1 : length]
            x32 = x_act.astype(F32)
            step_x = nn(step, spread, PRECISE) * x32
            tail = nn(jnp.exp(total - cum), spread, PRECISE)
            pay_out[:, b * inner : (b + 1) * inner] = tn(b_rows, (tail * step_x).astype(BF16)).astype(BF16)
            place = (iota((LANES, LANES), 1) == iota((LANES, LANES), 0) + b * heads) & (
                iota((LANES, LANES), 0) < heads
            )
            extra = extra + nn(jnp.exp(jnp.broadcast_to(total, (8, LANES))), place.astype(F32), PRECISE)[0:1]
            step_xb = step_x.astype(BF16)
            scores = nt(c_rows, b_rows)
            cum_t = cum.T
            for h in range(heads):
                decay = jnp.exp(jnp.where(causal, cum[:, h : h + 1] - cum_t[h : h + 1, :], -1e30))
                y_buf[:, h * head_size : (h + 1) * head_size] = nn(
                    (scores * decay).astype(BF16), step_xb[:, h * head_size : (h + 1) * head_size]
                )
            local_out[rows] = y_buf[...] + skip * x32
        high = extra.astype(BF16).astype(F32)
        low = pltpu.roll(jnp.broadcast_to(extra - high, (8, LANES)), LANES // 2, 1)[0:1]
        lane = iota((1, LANES), 1)
        both = jnp.where(lane < LANES // 2, high, low)
        pay_out[:, batch * inner :] = jnp.broadcast_to(both, (state, LANES)).astype(BF16)

    return kernel


def decay_rows(extra, width, head_size):
    pick = (iota((LANES, width), 0) % (LANES // 2) == iota((LANES, width), 1) // head_size).astype(BF16)
    return nn(extra, pick)


def scan_kernel(head_size, reverse):
    def kernel(part, decays, entering):
        peers, rows, width = entering.shape
        state = jnp.zeros((rows, width), F32)
        order = range(peers - 1, -1, -1) if reverse else range(peers)
        for peer in order:
            entering[peer] = state.astype(BF16)
            decay = decay_rows(decays[peer][:, decays.shape[2] - LANES :], width, head_size)
            state = decay * state + part[peer][:, :width].astype(F32)

    return kernel


def mix_kernel(dims, final):
    batch, length, inner, heads, head_size, state = dims

    def kernel(local, gate, prebc, cum, entered, gate_norm, *rest):
        if final:
            cot, w_out, mixed_out, q_out, sums_out = rest
        else:
            mixed_out, q_out = rest
        spread = spread_heads(inner, head_size)
        ones = jnp.ones((8, inner), F32)
        sums = jnp.zeros((8, length), F32)
        for b in range(batch):
            rows = slice(b * length, (b + 1) * length)
            pre = prebc[rows, state:]
            c_rows = (pre * sigmoid(pre)).astype(BF16)
            carried = nn(c_rows, entered[:, b * inner : (b + 1) * inner])
            mixed = local[rows] + nn(jnp.exp(cum[rows]), spread, PRECISE) * carried
            mixed_out[rows] = mixed
            g = gate[rows]
            gated = mixed * g * sigmoid(g)
            weighted = gated * gate_norm[...]
            q_out[rows] = weighted.astype(BF16)
            if final:
                grad = nt(cot[rows], w_out[...])
                row = iota((8, length), 0)
                sums = jnp.where(row == 2 * b, nt(ones, gated * gated, PRECISE), sums)
                sums = jnp.where(row == 2 * b + 1, nt(ones, grad * weighted, PRECISE), sums)
        if final:
            sums_out[...] = sums

    return kernel


def out_kernel(dims, peers, inner_total, last):
    batch, length, inner, heads, head_size, state = dims

    def kernel(stream, gain, *rest):
        q, w, gn = rest[:peers], rest[peers : 2 * peers], rest[2 * peers : 3 * peers]
        outs = rest[3 * peers :]
        for b in range(batch):
            rows = slice(b * length, (b + 1) * length)
            total = jnp.zeros((length, 1), F32)
            u = None
            for p in range(peers):
                part = q[p][rows]
                gated = part.astype(F32) / gn[p][...]
                total = total + jnp.sum(gated * gated, 1, keepdims=True)
                term = nn(part, w[p][...])
                u = term if u is None else u + term
            rstd = lax.rsqrt(total / inner_total + EPSILON)
            after = stream[rows].astype(F32) + rstd * u
            outs[0][rows] = after
            if not last:
                scale = lax.rsqrt(jnp.mean(after * after, 1, keepdims=True) + EPSILON)
                outs[1][rows] = (after * scale * gain[...]).astype(BF16)
                outs[2][rows] = u
                outs[3][rows] = jnp.broadcast_to(rstd, (length, LANES))

    return kernel


def gate_back_kernel(dims, inner_total, last, peers):
    batch, length, inner, heads, head_size, state = dims

    def kernel(grad_out, w_out, mixed, gate, prebc, cum, gate_norm, *rest):
        sources, (dmix_out, dgate_out, normed_out, pay_out, gn_out) = rest[:-5], rest[-5:]
        spread = spread_heads(inner, head_size)
        gn_grad = jnp.zeros((1, inner), F32)
        if last:
            sums = sources[0][...]
            for s in sources[1:]:
                sums = sums + s[...]
            eye = (iota((length, length), 0) == iota((length, length), 1)).astype(F32)
            columns = nt(eye, sums, PRECISE)
        for b in range(batch):
            rows = slice(b * length, (b + 1) * length)
            go = grad_out[rows]
            if last:
                rstd = lax.rsqrt(columns[:, 2 * b : 2 * b + 1] / inner_total + EPSILON)
                cross = columns[:, 2 * b + 1 : 2 * b + 2]
            else:
                u, rstd_in = sources
                rstd = rstd_in[rows, 0:1]
                cross = jnp.sum(go.astype(F32) * u[rows], 1, keepdims=True)
            grad = nt(go, w_out[...])
            g = gate[rows]
            sig = sigmoid(g)
            silu = g * sig
            mix = mixed[rows]
            gated = mix * silu
            gn = gate_norm[...]
            normed_out[rows] = (gated * rstd * gn).astype(BF16)
            gn_grad = gn_grad + jnp.sum(grad * gated * rstd, 0, keepdims=True)
            dgated = rstd * gn * grad - gated * (rstd * rstd * rstd * cross / inner_total)
            dmix = dgated * silu
            dmix_out[rows] = dmix
            dgate_out[rows] = (dgated * mix * sig * (1.0 + g * (1.0 - sig))).astype(BF16)
            pre = prebc[rows, state:]
            c_rows = (pre * sigmoid(pre)).astype(BF16)
            grown = nn(jnp.exp(cum[rows]), spread, PRECISE)
            pay_out[:, b * inner : (b + 1) * inner] = tn(c_rows, (grown * dmix).astype(BF16)).astype(BF16)
        gn_out[...] = jnp.broadcast_to(gn_grad, (8, inner))

    return kernel


def scan_back_kernel(dims):
    batch, length, inner, heads, head_size, state = dims

    def kernel(
        dmix, prex, prebc, padx, padbc, step_in, cum_in, entered, returned, head_par,
        gpx_out, gpbc_out, dstep_out, headx_out, headbc_out, tapx_out, tapbc_out, heads_out,
        dx_buf,
    ):
        spread = spread_heads(inner, head_size)
        upper = (iota((length, length), 0) <= iota((length, length), 1)).astype(F32)
        causal = iota((length, length), 0) >= iota((length, length), 1)
        rate = -jnp.exp(head_par[1:2])
        skip = nn(head_par[...], spread, PRECISE)[2:3]
        lane = iota((length, LANES), 1)
        sub = iota((LANES, length), 0)
        tap_rows = [[None] * 5, [None] * 5]
        head_rows = [jnp.zeros((1, LANES), F32)] * 3
        for b in range(batch):
            rows = slice(b * length, (b + 1) * length)
            cols = slice(b * inner, (b + 1) * inner)
            dy = dmix[rows]
            px, pbc = prex[rows], prebc[rows]
            sgx, sgbc = sigmoid(px), sigmoid(pbc)
            x_act = (px * sgx).astype(BF16)
            bc = (pbc * sgbc).astype(BF16)
            b_rows, c_rows = bc[:, :state], bc[:, state:]
            x32 = x_act.astype(F32)
            step_raw, cum = step_in[rows], cum_in[rows]
            step = softplus(step_raw)
            total = cum[length - 1 : length]
            step_rep = nn(step, spread, PRECISE)
            grown = nn(jnp.exp(cum), spread, PRECISE)
            tail = nn(jnp.exp(total - cum), spread, PRECISE)
            step_x = step_rep * x32
            step_xb = step_x.astype(BF16)
            dyb = dy.astype(BF16)
            s_in, g_in = entered[:, cols], returned[:, cols]
            scores = nt(c_rows, b_rows)
            cum_t = cum.T
            dscores = jnp.zeros((length, length), F32)
            by_row = jnp.zeros((length, LANES), F32)
            by_col = jnp.zeros((LANES, length), F32)
            for h in range(heads):
                own = slice(h * head_size, (h + 1) * head_size)
                decay = jnp.exp(jnp.where(causal, cum[:, h : h + 1] - cum_t[h : h + 1, :], -1e30))
                dx_buf[:, own] = tn((scores * decay).astype(BF16), dyb[:, own])
                part = nt(dyb[:, own], step_xb[:, own]) * decay
                dscores = dscores + part
                part = part * scores
                by_row = jnp.where(lane == h, jnp.sum(part, 1, keepdims=True), by_row)
                by_col = jnp.where(sub == h, jnp.sum(part, 0, keepdims=True), by_col)
            dscores = dscores.astype(BF16)
            back = nn(b_rows, g_in)
            tail_back = tail * back
            dstep_x = dx_buf[...] + tail_back
            into = grown * nn(c_rows, s_in)
            leave = nt(step_x * tail_back, spread, PRECISE)
            dcum = by_row - by_col.T + nt(dy * into, spread, PRECISE) - leave
            held = jnp.sum(s_in.astype(F32) * g_in.astype(F32), 0, keepdims=True)
            held = nt(jnp.broadcast_to(held, (8, inner)), spread, PRECISE)[0:1] * jnp.exp(total)
            last = held + jnp.sum(leave, 0, keepdims=True)
            dlog = nn(upper, dcum, PRECISE) + last
            dstep = nt(dstep_x * x32, spread, PRECISE) + rate * dlog
            draw = dstep * sigmoid(step_raw)
            dstep_out[rows] = draw.astype(BF16)
            head_rows[0] = head_rows[0] + jnp.sum(draw, 0, keepdims=True)
            head_rows[1] = head_rows[1] + jnp.sum(dlog * (rate * step), 0, keepdims=True)
            dskip = jnp.sum(dy * x32, 0, keepdims=True)
            head_rows[2] = head_rows[2] + nt(jnp.broadcast_to(dskip, (8, inner)), spread, PRECISE)[0:1]
            db = tn(dscores, c_rows) + nt((tail * step_x).astype(BF16), g_in)
            dc = nn(dscores, b_rows) + nt((grown * dy).astype(BF16), s_in)
            dx = step_rep * dstep_x + skip * dy
            gpx = dx * sgx * (1.0 + px * (1.0 - sgx))
            slope = sgbc * (1.0 + pbc * (1.0 - sgbc))
            gpx_out[rows] = gpx
            gpbc_out[rows, :state] = db * slope[:, :state]
            gpbc_out[rows, state:] = dc * slope[:, state:]
            gpbc = gpbc_out[rows]
            headx_out[b * 8 : (b + 1) * 8] = gpx[0:8]
            headbc_out[b * 8 : (b + 1) * 8] = gpbc[0:8]
            base = b * (length + 8)
            for which, (gp, pad) in enumerate(((gpx, padx), (gpbc, padbc))):
                for k in range(5):
                    term = gp if k == 4 else gp * pad[base + 5 + k : base + 5 + k + length]
                    term = jnp.sum(term, 0, keepdims=True)
                    old = tap_rows[which][k]
                    tap_rows[which][k] = term if old is None else old + term
        for out, terms in ((tapx_out, tap_rows[0]), (tapbc_out, tap_rows[1])):
            out[...] = jnp.zeros_like(out)
            for k in range(5):
                out[k : k + 1] = terms[k]
        heads_out[...] = jnp.zeros_like(heads_out)
        for k in range(3):
            heads_out[k : k + 1] = head_rows[k]

    return kernel


def conv_back_kernel(dims):
    batch, length, inner, heads, head_size, state = dims

    def kernel(
        gpx, gpbc, aheadx, aheadbc, taps_x, taps_bc, dgate, dstep, w_gate, w_val, w_bc, w_dt,
        grx_out, grbc_out, part_out, extx, extbc,
    ):
        for b in range(batch):
            rows = slice(b * length, (b + 1) * length)
            part = nt(dgate[rows], w_gate[...]) + nt(dstep[rows], w_dt[...])
            for gp, ahead, taps, ext, weight, out in (
                (gpx, aheadx, taps_x, extx, w_val, grx_out),
                (gpbc, aheadbc, taps_bc, extbc, w_bc, grbc_out),
            ):
                ext[0:length] = gp[rows]
                ext[length : length + 8] = ahead[b * 8 : (b + 1) * 8]
                grad = taps[3:4] * ext[0:length]
                for k in range(3):
                    grad = grad + taps[k : k + 1] * ext[3 - k : 3 - k + length]
                grad = grad.astype(BF16)
                out[rows] = grad
                part = part + nt(grad, weight[...])
            part_out[rows] = part.astype(BF16)

    return kernel


def weight_kernel(normed, dgate, grx, grbc, dstep, normed_out, grad_out, zg_out, zv_out, bc_out, dt_out, wo_out):
    x = normed[...]
    zg_out[...] = tn(x, dgate[...]).astype(BF16)
    zv_out[...] = tn(x, grx[...]).astype(BF16)
    bc_out[...] = tn(x, grbc[...]).astype(BF16)
    dt_out[...] = tn(dstep[...], x)[: dt_out.shape[0]].astype(BF16)
    wo_out[...] = tn(normed_out[...], grad_out[...]).astype(BF16)


def norm_back_kernel(width):
    def kernel(place, parts, stream, residual, gain, grad_out, gain_out):
        total = parts[0].astype(F32)
        for p in range(1, parts.shape[0]):
            total = total + parts[p].astype(F32)
        x = stream[...].astype(F32)
        rstd = lax.rsqrt(jnp.mean(x * x, 1, keepdims=True) + EPSILON)
        gain_out[...] = jnp.broadcast_to(jnp.sum(total * x * rstd, 0, keepdims=True), gain_out.shape)
        weighted = total * gain[...]
        dot = jnp.sum(weighted * x, 1, keepdims=True)
        grad = rstd * weighted - x * (rstd * rstd * rstd * dot / width) + residual[...].astype(F32)
        grad_out[...] = grad.astype(BF16)

    return kernel


def shifted(shard, axis, by):
    peers = lax.axis_size(axis)
    pairs = [(i, i + by) for i in range(peers) if 0 <= i + by < peers]
    return lax.ppermute(shard, axis, pairs)


def gather_pieces(shard, axis):
    peers = lax.axis_size(axis)
    return [shard] + [
        lax.ppermute(shard, axis, [(i, i ^ s) for i in range(peers)]) for s in range(1, peers)
    ]


def swap(blocks, axis):
    return lax.all_to_all(blocks, axis, 0, 0)


def shards(
    hidden, cotangent, norm_gain, w_in_zx, w_in_dt, w_in_bc, conv_x, conv_x_bias, conv_bc,
    conv_bc_bias, dt_bias, a_log, d_skip, gate_norm, w_out,
):
    batch, length, width = hidden.shape
    rows = batch * length
    peers = lax.axis_size("head")
    ranks = lax.axis_size("seq")
    share = rows // peers
    layers, inner = w_out.shape[:2]
    heads = dt_bias.shape[1]
    head_size = inner // heads
    state = w_in_bc.shape[2] // 2
    inner_total = inner * peers
    dims = (batch, length, inner, heads, head_size, state)
    place = lax.axis_index("head").astype(jnp.int32).reshape(1)

    hidden_rows = hidden.reshape(rows, width)
    cot_rows = cotangent.reshape(rows, width)
    w_zx = jnp.transpose(w_in_zx, (0, 2, 1, 3))
    w_dt = jnp.pad(w_in_dt, ((0, 0), (0, 0), (0, LANES - heads)))
    head_par = jnp.pad(jnp.stack([dt_bias, a_log, d_skip], 1), ((0, 0), (0, 5), (0, LANES - heads)))
    taps_x = jnp.pad(jnp.concatenate([conv_x, conv_x_bias[:, None]], 1), ((0, 0), (0, 3), (0, 0)))
    taps_bc = jnp.pad(jnp.concatenate([conv_bc, conv_bc_bias[:, None]], 1), ((0, 0), (0, 3), (0, 0)))
    gates = gate_norm[:, None]
    gains = norm_gain[:, None]

    def norm_low(x, gain):
        x = x.astype(F32)
        return (x * lax.rsqrt(jnp.mean(x * x, -1, keepdims=True) + EPSILON) * gain).astype(BF16)

    hidden_halo = shifted(hidden[:, length - HALO :], "seq", 1)
    gate_pieces = gather_pieces(jnp.broadcast_to(gates, (layers, 8, inner)), "head")
    out_pieces = [gather_pieces(w_out[0], "head"), None]
    normed = norm_low(hidden_rows, norm_gain[0])
    halo = norm_low(hidden_halo, norm_gain[0]).reshape(batch * HALO, width)
    stream = hidden_rows
    saved = []
    for l in range(layers):
        last = l == layers - 1
        sub = lambda a, extra=None: layer_spec(a, l, extra)
        pad = batch * (length + 8)
        gate, padx, padbc, prex, prebc, local, step, cum, pay = call(
            forward_kernel(dims),
            [
                ((rows, inner), F32), ((pad, inner), F32), ((pad, 2 * state), F32),
                ((rows, inner), F32), ((rows, 2 * state), F32), ((rows, inner), F32),
                ((rows, LANES), F32), ((rows, LANES), F32), ((state, batch * inner + LANES), BF16),
            ],
            [normed, halo, w_zx, w_zx, w_in_bc, w_dt, taps_x, taps_bc, head_par],
            [None, None, sub(w_zx, 0), sub(w_zx, 1), sub(w_in_bc), sub(w_dt), sub(taps_x), sub(taps_bc),
             sub(head_par)],
            [pltpu.VMEM((length, inner), F32)],
        )
        parts = swap(pay.reshape(ranks, state // ranks, batch * inner + LANES), "seq")
        entered = call(
            scan_kernel(head_size, False),
            [((ranks, state // ranks, batch * inner), BF16)],
            [parts, parts],
        )[0]
        entered = swap(entered, "seq").reshape(state, batch * inner)
        kept = dict(
            normed=normed, stream=stream, gate=gate, padx=padx, padbc=padbc, prex=prex, prebc=prebc,
            step=step, cum=cum, parts=parts, entered=entered,
        )
        args = [local, gate, prebc, cum, entered, gates]
        specs = [None] * 5 + [sub(gates)]
        outs = [((rows, inner), F32), ((rows, inner), BF16)]
        if last:
            args += [cot_rows, w_out]
            specs += [None, sub(w_out)]
            outs += [((8, length), F32)]
        mixed, q, *sums = call(mix_kernel(dims, last), outs, args, specs)
        kept["mixed"] = mixed
        if last:
            kept["sources"] = gather_pieces(sums[0], "head")
        qs = gather_pieces(q, "head")
        outs = [((rows, width), F32)]
        if not last:
            outs += [((rows, width), BF16), ((rows, width), F32), ((rows, LANES), F32)]
        gain_next = min(l + 1, layers - 1)
        piece_specs = [layer_spec(g[:, :1], l) for g in gate_pieces]
        after = call(
            out_kernel(dims, peers, inner_total, last),
            outs,
            [stream, gains, *qs, *out_pieces[l], *[g[:, :1] for g in gate_pieces]],
            [None, layer_spec(gains, gain_next)] + [None] * (2 * peers) + piece_specs,
        )
        if last:
            final_out = after[0]
        else:
            stream, normed, u, rstd = after
            kept["sources"] = [u, rstd]
            halo = shifted(normed.reshape(batch, length, width)[:, length - HALO :], "seq", 1)
            halo = halo.reshape(batch * HALO, width)
            held, normed = lax.optimization_barrier((w_out[l + 1], normed))
            out_pieces[l + 1] = gather_pieces(held, "head")
        saved.append(kept)

    grad = cot_rows
    done = [None] * layers
    gain_rows = [None] * layers
    for l in range(layers - 1, -1, -1):
        last = l == layers - 1
        sub = lambda a, extra=None: layer_spec(a, l, extra)
        kept = saved[l]
        sources = kept["sources"]
        dmix, dgate, kept_out, pay, gn_grad = call(
            gate_back_kernel(dims, inner_total, last, peers),
            [((rows, inner), F32), ((rows, inner), BF16), ((rows, inner), BF16),
             ((state, batch * inner), BF16), ((8, inner), F32)],
            [grad, w_out, kept["mixed"], kept["gate"], kept["prebc"], kept["cum"], gates, *sources],
            [None, sub(w_out), None, None, None, None, sub(gates)] + [None] * len(sources),
        )
        back = swap(pay.reshape(ranks, state // ranks, batch * inner), "seq")
        returned = call(
            scan_kernel(head_size, True),
            [((ranks, state // ranks, batch * inner), BF16)],
            [back, kept["parts"]],
        )[0]
        returned = swap(returned, "seq").reshape(state, batch * inner)
        gpx, gpbc, dstep, headx, headbc, tapx, tapbc, head_grads = call(
            scan_back_kernel(dims),
            [((rows, inner), F32), ((rows, 2 * state), F32), ((rows, LANES), BF16),
             ((batch * 8, inner), F32), ((batch * 8, 2 * state), F32),
             ((8, inner), F32), ((8, 2 * state), F32), ((8, LANES), F32)],
            [dmix, kept["prex"], kept["prebc"], kept["padx"], kept["padbc"], kept["step"], kept["cum"],
             kept["entered"], returned, head_par],
            [None] * 9 + [sub(head_par)],
            [pltpu.VMEM((length, inner), F32)],
        )
        aheadx = shifted(headx, "seq", -1)
        aheadbc = shifted(headbc, "seq", -1)
        grx, grbc, part = call(
            conv_back_kernel(dims),
            [((rows, inner), BF16), ((rows, 2 * state), BF16), ((rows, width), BF16)],
            [gpx, gpbc, aheadx, aheadbc, taps_x, taps_bc, dgate, dstep, w_zx, w_zx, w_in_bc, w_dt],
            [None] * 4 + [sub(taps_x), sub(taps_bc), None, None, sub(w_zx, 0), sub(w_zx, 1), sub(w_in_bc),
                          sub(w_dt)],
            [pltpu.VMEM((length + 8, inner), F32), pltpu.VMEM((length + 8, 2 * state), F32)],
        )
        grad_in = grad
        parts = swap(part.reshape(peers, share, width), "head")
        grad_share, gain_grad = call(
            norm_back_kernel(width),
            [((share, width), BF16), ((8, width), F32)],
            [parts, kept["stream"], grad, gains],
            [None] + [pl.BlockSpec((share, width), lambda _, at: (at[0], 0))] * 2 + [sub(gains)],
            prefetch=place,
        )
        grad = lax.all_gather(grad_share, "head", axis=0, tiled=True)
        gain_rows[l] = gain_grad[0]
        head_rows = -(-heads // 8) * 8
        zg, zv, bc, dt, wo = call(
            weight_kernel,
            [((width, inner), BF16), ((width, inner), BF16), ((width, 2 * state), BF16),
             ((head_rows, width), BF16), ((inner, width), BF16)],
            [kept["normed"], dgate, grx, grbc, dstep, kept_out, grad_in],
        )
        bc_total = width + 8
        bc_rows = -(-bc_total // (16 * peers)) * 16 * peers
        packed = jnp.concatenate(
            [bc, tapbc.astype(BF16), jnp.zeros((bc_rows - bc_total, 2 * state), BF16)], 0
        )
        packed = swap(packed.reshape(peers, bc_rows // peers, 2 * state), "head")
        packed = jnp.sum(packed.astype(F32), 0).astype(BF16)
        small = jnp.concatenate([tapx, gn_grad, jnp.pad(head_grads, ((0, 0), (0, width - LANES)))[:, :inner]], 0)
        zg, zv, wo, dt, packed, small = lax.psum((zg, zv, wo, dt, packed, small.astype(BF16)), "seq")
        packed = lax.all_gather(packed, "head", axis=0, tiled=True).astype(F32)
        small = small.astype(F32)
        done[l] = dict(
            zx=jnp.stack([zg, zv], 1).astype(F32),
            dt=dt[:heads].T.astype(F32),
            bc=packed[:width],
            conv_x=small[:4],
            conv_x_bias=small[4],
            conv_bc=packed[width : width + 4],
            conv_bc_bias=packed[width + 4],
            dt_bias=small[16, :heads],
            a_log=small[17, :heads],
            d_skip=small[18, :heads],
            gate_norm=small[8],
            wo=wo.astype(F32),
        )
    gain_sum = sum(gather_pieces(jnp.stack(gain_rows), "head"))
    hop = 1
    while hop < ranks:
        gain_sum = gain_sum + lax.ppermute(gain_sum, "seq", [(i, i ^ hop) for i in range(ranks)])
        hop *= 2
    both = lambda name: jnp.stack([d[name] for d in done])
    return (
        final_out.reshape(hidden.shape),
        grad.astype(F32).reshape(hidden.shape),
        gain_sum,
        both("zx"),
        both("dt"),
        both("bc"),
        both("conv_x"),
        both("conv_x_bias"),
        both("conv_bc"),
        both("conv_bc_bias"),
        both("dt_bias"),
        both("a_log"),
        both("d_skip"),
        both("gate_norm"),
        both("wo"),
    )


def solution(mesh):
    tokens = P(None, "seq", None)
    heads = P(None, "head")
    last = P(None, None, "head")
    placed = (
        tokens, tokens, P(), P(None, None, None, "head"), last, P(), last, heads, P(), P(), heads, heads,
        heads, heads, P(None, "head", None),
    )
    results = (
        tokens, tokens, P(), P(None, None, None, "head"), last, P(), last, heads, P(), P(), heads, heads,
        heads, heads, P(None, "head", None),
    )
    return jax.shard_map(shards, mesh=mesh, in_specs=placed, out_specs=results, check_vma=False)
```

```python
import math

import jax
import jax.numpy as jnp
from jax import lax
from jax.experimental import pallas as pl
from jax.experimental.pallas import tpu as pltpu
from jax.sharding import PartitionSpec as P

EPSILON = 1e-05
PRECISE = lax.Precision.HIGHEST
LANES = 128
HALO = 16
F32 = jnp.float32
BF16 = jnp.bfloat16


def nn(a, b, precision=None):
    return lax.dot_general(
        a, b, (((1,), (0,)), ((), ())), precision=precision, preferred_element_type=F32
    )


def nt(a, b, precision=None):
    return lax.dot_general(
        a, b, (((1,), (1,)), ((), ())), precision=precision, preferred_element_type=F32
    )


def tn(a, b, precision=None):
    return lax.dot_general(
        a, b, (((0,), (0,)), ((), ())), precision=precision, preferred_element_type=F32
    )


def iota(shape, axis):
    return lax.broadcasted_iota(jnp.int32, shape, axis)


def sigmoid(v):
    return 1.0 / (1.0 + jnp.exp(-v))


def softplus(v):
    small = jnp.exp(-jnp.abs(v))
    grown = 1.0 + small
    gap = grown - 1.0
    log1p = jnp.where(gap == 0.0, small, jnp.log(grown) * small / jnp.where(gap == 0.0, 1.0, gap))
    return jnp.maximum(v, 0.0) + log1p


def spread_heads(inner, head_size):
    return (iota((LANES, inner), 1) // head_size == iota((LANES, inner), 0)).astype(F32)


def two_parts(column):
    high = column.astype(BF16).astype(F32)
    lane = iota((column.shape[0], LANES), 1)
    return jnp.where(lane == 0, high, jnp.where(lane == 1, column - high, 0.0)).astype(BF16)


def lower_tri(length):
    return (iota((length, length), 0) >= iota((length, length), 1)).astype(F32)


def call(kernel, outs, args, specs=None, scratch=(), prefetch=None):
    whole = lambda a: pl.BlockSpec(a.shape, lambda *_, n=a.ndim: (0,) * n)
    in_specs = [whole(a) if s is None else s for a, s in zip(args, specs or [None] * len(args))]
    out_shape = [jax.ShapeDtypeStruct(s, d) for s, d in outs]
    return pl.pallas_call(
        kernel,
        grid_spec=pltpu.PrefetchScalarGridSpec(
            num_scalar_prefetch=0 if prefetch is None else 1,
            grid=(1,),
            in_specs=in_specs,
            out_specs=[whole(o) for o in out_shape],
            scratch_shapes=list(scratch),
        ),
        out_shape=out_shape,
    )(*(() if prefetch is None else (prefetch,)), *args)


def layer_spec(array, layer, extra=None):
    shape = (None,) + array.shape[1:]
    index = (layer,) + (0,) * (array.ndim - 1)
    if extra is not None:
        shape = (None, None) + array.shape[2:]
        index = (layer, extra) + (0,) * (array.ndim - 2)
    return pl.BlockSpec(shape, lambda *_: index)


def forward_kernel(dims):
    batch, length, inner, heads, head_size, state = dims

    def kernel(
        normed, halo, w_gate, w_val, w_bc, w_dt, taps_x, taps_bc, head_par,
        gate_out, padx_out, padbc_out, prex_out, prebc_out, step_out, cum_out, pay_out,
    ):
        spread = spread_heads(inner, head_size)
        tri = lower_tri(length)
        rates = -jnp.exp(head_par[1:2])
        width = w_gate.shape[0]
        extra = jnp.zeros((1, LANES), F32)
        for b in range(batch):
            rows = slice(b * length, (b + 1) * length)
            x_in = normed[rows, :width]
            x_halo = halo[b * HALO : (b + 1) * HALO, :width]
            gate_out[rows] = nn(x_in, w_gate[...])
            acts = []
            for weight, taps, pad_out, pre_out in (
                (w_val, taps_x, padx_out, prex_out),
                (w_bc, taps_bc, padbc_out, prebc_out),
            ):
                base = b * (length + 8)
                pad_out[base : base + 8] = nn(x_halo, weight[...])[HALO - 8 :].astype(BF16).astype(F32)
                pad_out[base + 8 : base + 8 + length] = nn(x_in, weight[...]).astype(BF16).astype(F32)
                pre = taps[4:5] + taps[0:1] * pad_out[base + 5 : base + 5 + length]
                for k in range(1, 4):
                    pre = pre + taps[k : k + 1] * pad_out[base + 5 + k : base + 5 + k + length]
                pre_out[rows] = pre
                acts.append((pre * sigmoid(pre)).astype(BF16))
            x_act, bc = acts
            b_rows = bc[:, :state]
            step_raw = nn(x_in, w_dt[...]) + head_par[0:1]
            step = softplus(step_raw)
            cum = nn(tri, rates * step, PRECISE)
            step_out[rows] = step_raw
            cum_out[rows] = cum
            total = cum[length - 1 : length]
            x32 = x_act.astype(F32)
            step_x = nn(step, spread, PRECISE) * x32
            tail = nn(jnp.exp(total - cum), spread, PRECISE)
            pay_out[:, b * inner : (b + 1) * inner] = tn(b_rows, (tail * step_x).astype(BF16)).astype(BF16)
            place = (iota((LANES, LANES), 1) == iota((LANES, LANES), 0) + b * heads) & (
                iota((LANES, LANES), 0) < heads
            )
            extra = extra + nn(jnp.exp(jnp.broadcast_to(total, (8, LANES))), place.astype(F32), PRECISE)[0:1]
        high = extra.astype(BF16).astype(F32)
        low = pltpu.roll(jnp.broadcast_to(extra - high, (8, LANES)), LANES // 2, 1)[0:1]
        lane = iota((1, LANES), 1)
        both = jnp.where(lane < LANES // 2, high, low)
        pay_out[:, batch * inner :] = jnp.broadcast_to(both, (state, LANES)).astype(BF16)

    return kernel


def local_kernel(dims):
    batch, length, inner, heads, head_size, state = dims

    def kernel(prex, prebc, step_in, cum_in, head_par, local_out, y_buf):
        spread = spread_heads(inner, head_size)
        causal = iota((length, length), 0) >= iota((length, length), 1)
        skip = nn(head_par[...], spread, PRECISE)[2:3]
        for b in range(batch):
            rows = slice(b * length, (b + 1) * length)
            px, pbc = prex[rows], prebc[rows]
            x32 = (px * sigmoid(px)).astype(BF16).astype(F32)
            bc = (pbc * sigmoid(pbc)).astype(BF16)
            cum = cum_in[rows]
            step_xb = (nn(softplus(step_in[rows]), spread, PRECISE) * x32).astype(BF16)
            scores = nt(bc[:, state:], bc[:, :state])
            cum_t = cum.T
            for h in range(heads):
                own = slice(h * head_size, (h + 1) * head_size)
                decay = jnp.exp(jnp.where(causal, cum[:, h : h + 1] - cum_t[h : h + 1, :], -1e30))
                y_buf[:, own] = nn((scores * decay).astype(BF16), step_xb[:, own])
            local_out[rows] = y_buf[...] + skip * x32

    return kernel


def decay_rows(extra, width, head_size):
    pick = (iota((LANES, width), 0) % (LANES // 2) == iota((LANES, width), 1) // head_size).astype(BF16)
    return nn(extra, pick)


def scan_kernel(head_size, reverse):
    def kernel(part, decays, entering):
        peers, rows, width = entering.shape
        state = jnp.zeros((rows, width), F32)
        order = range(peers - 1, -1, -1) if reverse else range(peers)
        for peer in order:
            entering[peer] = state.astype(BF16)
            decay = decay_rows(decays[peer][:, decays.shape[2] - LANES :], width, head_size)
            state = decay * state + part[peer][:, :width].astype(F32)

    return kernel


def mix_kernel(dims, final):
    batch, length, inner, heads, head_size, state = dims

    def kernel(local, gate, prebc, cum, entered, gate_norm, w_out, *rest):
        if final:
            cot, mixed_out, branch_out, sums_out = rest
        else:
            mixed_out, branch_out = rest
        width = w_out.shape[1]
        spread = spread_heads(inner, head_size)
        ones = jnp.ones((8, inner), F32)
        sums = jnp.zeros((8, length), F32)
        for b in range(batch):
            rows = slice(b * length, (b + 1) * length)
            pre = prebc[rows, state:]
            c_rows = (pre * sigmoid(pre)).astype(BF16)
            carried = nn(c_rows, entered[:, b * inner : (b + 1) * inner])
            mixed = local[rows] + nn(jnp.exp(cum[rows]), spread, PRECISE) * carried
            mixed_out[rows] = mixed
            g = gate[rows]
            gated = mixed * g * sigmoid(g)
            weighted = gated * gate_norm[...]
            branch_out[rows, :width] = nn(weighted.astype(BF16), w_out[...]).astype(BF16)
            if not final:
                branch_out[rows, width:] = two_parts(jnp.sum(gated * gated, 1, keepdims=True))
            if final:
                grad = nt(cot[rows], w_out[...])
                row = iota((8, length), 0)
                sums = jnp.where(row == 2 * b, nt(ones, gated * gated, PRECISE), sums)
                sums = jnp.where(row == 2 * b + 1, nt(ones, grad * weighted, PRECISE), sums)
        if final:
            sums_out[...] = sums

    return kernel


def join_kernel(inner_total):
    def kernel(place, parts, stream, gain, after_out, low_out, u_out):
        total = parts[0].astype(F32)
        for p in range(1, parts.shape[0]):
            total = total + parts[p].astype(F32)
        width = stream.shape[1]
        u = total[:, :width]
        square = jnp.sum(total[:, width:], 1, keepdims=True)
        rstd = lax.rsqrt(square / inner_total + EPSILON)
        after = stream[...].astype(F32) + rstd * u
        after_out[...] = after
        scale = lax.rsqrt(jnp.mean(after * after, 1, keepdims=True) + EPSILON)
        low_out[:, :width] = (after * scale * gain[...]).astype(BF16)
        low_out[:, width:] = two_parts(rstd)
        u_out[...] = u

    return kernel


def final_kernel(place, branch, stream, rstd, out):
    out[...] = (stream[...].astype(F32) + rstd[:, 0:1] * branch[...].astype(F32)).astype(BF16)


def gate_back_kernel(dims, inner_total, last, peers):
    batch, length, inner, heads, head_size, state = dims

    def kernel(grad_out, w_out, mixed, gate, prebc, cum, gate_norm, *rest):
        if last:
            rest, rstd_out = rest[:-1], rest[-1]
        sources, (dmix_out, dgate_out, normed_out, pay_out, gn_out) = rest[:-5], rest[-5:]
        spread = spread_heads(inner, head_size)
        width = w_out.shape[1]
        gn_grad = jnp.zeros((1, inner), F32)
        if last:
            sums = sources[0][...]
            for s in sources[1:]:
                sums = sums + s[...]
            eye = (iota((length, length), 0) == iota((length, length), 1)).astype(F32)
            columns = nt(eye, sums, PRECISE)
        for b in range(batch):
            rows = slice(b * length, (b + 1) * length)
            go = grad_out[rows, :width]
            if last:
                rstd = lax.rsqrt(columns[:, 2 * b : 2 * b + 1] / inner_total + EPSILON)
                cross = columns[:, 2 * b + 1 : 2 * b + 2]
                rstd_out[rows] = jnp.broadcast_to(rstd, (length, LANES))
            else:
                rstd = jnp.sum(sources[0][rows, width:].astype(F32), 1, keepdims=True)
                cross = jnp.sum(grad_out[rows, width:].astype(F32), 1, keepdims=True)
            grad = nt(go, w_out[...])
            g = gate[rows]
            sig = sigmoid(g)
            silu = g * sig
            mix = mixed[rows]
            gated = mix * silu
            gn = gate_norm[...]
            normed_out[rows] = (gated * rstd * gn).astype(BF16)
            gn_grad = gn_grad + jnp.sum(grad * gated * rstd, 0, keepdims=True)
            dgated = rstd * gn * grad - gated * (rstd * rstd * rstd * cross / inner_total)
            dmix = dgated * silu
            dmix_out[rows] = dmix
            dgate_out[rows] = (dgated * mix * sig * (1.0 + g * (1.0 - sig))).astype(BF16)
            pre = prebc[rows, state:]
            c_rows = (pre * sigmoid(pre)).astype(BF16)
            grown = nn(jnp.exp(cum[rows]), spread, PRECISE)
            pay_out[:, b * inner : (b + 1) * inner] = tn(c_rows, (grown * dmix).astype(BF16)).astype(BF16)
        gn_out[...] = jnp.broadcast_to(gn_grad, (8, inner))

    return kernel


def local_back_kernel(dims):
    batch, length, inner, heads, head_size, state = dims

    def kernel(dmix, prex, prebc, step_in, cum_in, dx_out, dbc_out, dcum_out, dx_buf):
        spread = spread_heads(inner, head_size)
        causal = iota((length, length), 0) >= iota((length, length), 1)
        lane = iota((length, LANES), 1)
        sub = iota((LANES, length), 0)
        for b in range(batch):
            rows = slice(b * length, (b + 1) * length)
            px, pbc = prex[rows], prebc[rows]
            x32 = (px * sigmoid(px)).astype(BF16).astype(F32)
            bc = (pbc * sigmoid(pbc)).astype(BF16)
            b_rows, c_rows = bc[:, :state], bc[:, state:]
            cum = cum_in[rows]
            step_xb = (nn(softplus(step_in[rows]), spread, PRECISE) * x32).astype(BF16)
            dyb = dmix[rows].astype(BF16)
            scores = nt(c_rows, b_rows)
            cum_t = cum.T
            dscores = jnp.zeros((length, length), F32)
            by_row = jnp.zeros((length, LANES), F32)
            by_col = jnp.zeros((LANES, length), F32)
            for h in range(heads):
                own = slice(h * head_size, (h + 1) * head_size)
                decay = jnp.exp(jnp.where(causal, cum[:, h : h + 1] - cum_t[h : h + 1, :], -1e30))
                dx_buf[:, own] = tn((scores * decay).astype(BF16), dyb[:, own])
                part = nt(dyb[:, own], step_xb[:, own]) * decay
                dscores = dscores + part
                part = part * scores
                by_row = jnp.where(lane == h, jnp.sum(part, 1, keepdims=True), by_row)
                by_col = jnp.where(sub == h, jnp.sum(part, 0, keepdims=True), by_col)
            dscores = dscores.astype(BF16)
            dx_out[rows] = dx_buf[...]
            dbc_out[rows, :state] = tn(dscores, c_rows)
            dbc_out[rows, state:] = nn(dscores, b_rows)
            dcum_out[rows] = by_row - by_col.T

    return kernel


def scan_back_kernel(dims):
    batch, length, inner, heads, head_size, state = dims

    def kernel(
        dmix, prex, prebc, padx, padbc, step_in, cum_in, entered, returned, head_par,
        dx_local, dbc_local, dcum_local,
        gpx_out, gpbc_out, dstep_out, headx_out, headbc_out, tapx_out, tapbc_out, heads_out,
    ):
        spread = spread_heads(inner, head_size)
        upper = (iota((length, length), 0) <= iota((length, length), 1)).astype(F32)
        rate = -jnp.exp(head_par[1:2])
        skip = nn(head_par[...], spread, PRECISE)[2:3]
        tap_rows = [[None] * 5, [None] * 5]
        head_rows = [jnp.zeros((1, LANES), F32)] * 3
        for b in range(batch):
            rows = slice(b * length, (b + 1) * length)
            cols = slice(b * inner, (b + 1) * inner)
            dy = dmix[rows]
            px, pbc = prex[rows], prebc[rows]
            sgx, sgbc = sigmoid(px), sigmoid(pbc)
            x_act = (px * sgx).astype(BF16)
            bc = (pbc * sgbc).astype(BF16)
            b_rows, c_rows = bc[:, :state], bc[:, state:]
            x32 = x_act.astype(F32)
            step_raw, cum = step_in[rows], cum_in[rows]
            step = softplus(step_raw)
            total = cum[length - 1 : length]
            step_rep = nn(step, spread, PRECISE)
            grown = nn(jnp.exp(cum), spread, PRECISE)
            tail = nn(jnp.exp(total - cum), spread, PRECISE)
            step_x = step_rep * x32
            s_in, g_in = entered[:, cols], returned[:, cols]
            back = nn(b_rows, g_in)
            tail_back = tail * back
            dstep_x = dx_local[rows] + tail_back
            into = grown * nn(c_rows, s_in)
            leave = nt(step_x * tail_back, spread, PRECISE)
            dcum = dcum_local[rows] + nt(dy * into, spread, PRECISE) - leave
            held = jnp.sum(s_in.astype(F32) * g_in.astype(F32), 0, keepdims=True)
            held = nt(jnp.broadcast_to(held, (8, inner)), spread, PRECISE)[0:1] * jnp.exp(total)
            last = held + jnp.sum(leave, 0, keepdims=True)
            dlog = nn(upper, dcum, PRECISE) + last
            dstep = nt(dstep_x * x32, spread, PRECISE) + rate * dlog
            draw = dstep * sigmoid(step_raw)
            dstep_out[rows] = draw.astype(BF16)
            head_rows[0] = head_rows[0] + jnp.sum(draw, 0, keepdims=True)
            head_rows[1] = head_rows[1] + jnp.sum(dlog * (rate * step), 0, keepdims=True)
            dskip = jnp.sum(dy * x32, 0, keepdims=True)
            head_rows[2] = head_rows[2] + nt(jnp.broadcast_to(dskip, (8, inner)), spread, PRECISE)[0:1]
            db = dbc_local[rows, :state] + nt((tail * step_x).astype(BF16), g_in)
            dc = dbc_local[rows, state:] + nt((grown * dy).astype(BF16), s_in)
            dx = step_rep * dstep_x + skip * dy
            gpx = dx * sgx * (1.0 + px * (1.0 - sgx))
            slope = sgbc * (1.0 + pbc * (1.0 - sgbc))
            gpx_out[rows] = gpx
            gpbc_out[rows, :state] = db * slope[:, :state]
            gpbc_out[rows, state:] = dc * slope[:, state:]
            gpbc = gpbc_out[rows]
            headx_out[b * 8 : (b + 1) * 8] = gpx[0:8]
            headbc_out[b * 8 : (b + 1) * 8] = gpbc[0:8]
            base = b * (length + 8)
            for which, (gp, pad) in enumerate(((gpx, padx), (gpbc, padbc))):
                for k in range(5):
                    term = gp if k == 4 else gp * pad[base + 5 + k : base + 5 + k + length]
                    term = jnp.sum(term, 0, keepdims=True)
                    old = tap_rows[which][k]
                    tap_rows[which][k] = term if old is None else old + term
        for out, terms in ((tapx_out, tap_rows[0]), (tapbc_out, tap_rows[1])):
            out[...] = jnp.zeros_like(out)
            for k in range(5):
                out[k : k + 1] = terms[k]
        heads_out[...] = jnp.zeros_like(heads_out)
        for k in range(3):
            heads_out[k : k + 1] = head_rows[k]

    return kernel


def conv_back_kernel(dims):
    batch, length, inner, heads, head_size, state = dims

    def kernel(
        gpx, gpbc, aheadx, aheadbc, taps_x, taps_bc, dgate, dstep, w_gate, w_val, w_bc, w_dt,
        grx_out, grbc_out, part_out, extx, extbc,
    ):
        for b in range(batch):
            rows = slice(b * length, (b + 1) * length)
            part = nt(dgate[rows], w_gate[...]) + nt(dstep[rows], w_dt[...])
            for gp, ahead, taps, ext, weight, out in (
                (gpx, aheadx, taps_x, extx, w_val, grx_out),
                (gpbc, aheadbc, taps_bc, extbc, w_bc, grbc_out),
            ):
                ext[0:length] = gp[rows]
                ext[length : length + 8] = ahead[b * 8 : (b + 1) * 8]
                grad = taps[3:4] * ext[0:length]
                for k in range(3):
                    grad = grad + taps[k : k + 1] * ext[3 - k : 3 - k + length]
                grad = grad.astype(BF16)
                out[rows] = grad
                part = part + nt(grad, weight[...])
            part_out[rows] = part.astype(BF16)

    return kernel


def early_weights_kernel(normed, dgate, normed_out, grad_out, gn_grad, zg_out, wo_out):
    width, inner = wo_out.shape[1], wo_out.shape[0]
    zg_out[0:width] = tn(normed[:, :width], dgate[...]).astype(BF16)
    zg_out[width : width + 16] = jnp.concatenate([gn_grad[...], gn_grad[...]], 0).astype(BF16)
    wo_out[...] = tn(normed_out[...], grad_out[:, :width]).astype(BF16)


def late_weights_kernel(heads_high, width, packed):
    def kernel(normed, grx, grbc, dstep, tapx, tapbc, head_grads, *rest):
        if packed:
            bc_before, pack_out, zv_out, bc_out = rest
        else:
            zv_out, bc_out = rest
        inner, both = zv_out.shape[1], bc_out.shape[1]
        x = normed[:, :width]
        zv_out[0:width] = tn(x, grx[...]).astype(BF16)
        zv_out[width : width + 8] = tapx[...].astype(BF16)
        zv_out[width + 8 :] = jnp.zeros((zv_out.shape[0] - width - 8, inner), BF16)
        zv_out[width + 8 : width + 16, :LANES] = head_grads[...].astype(BF16)
        steps = tn(dstep[...], x)[:heads_high].astype(BF16)
        for k in range(width // inner):
            low = width + 16 + k * heads_high
            zv_out[low : low + heads_high] = steps[:, k * inner : (k + 1) * inner]
        bc_out[0:width] = tn(x, grbc[...]).astype(BF16)
        bc_out[width : width + 8] = tapbc[...].astype(BF16)
        bc_out[width + 8 :] = jnp.zeros((bc_out.shape[0] - width - 8, both), BF16)
        if packed:
            bc_out[width + 16 : 2 * width + 32] = bc_before[...]
            ranks, _, lanes = pack_out.shape
            low = 0
            for source in (zv_out, bc_out):
                high = source.shape[0] // ranks
                for c in range(source.shape[1] // lanes):
                    for j in range(ranks):
                        pack_out[j, low : low + high] = source[
                            j * high : (j + 1) * high, c * lanes : (c + 1) * lanes
                        ]
                    low += high

    return kernel


def norm_back_kernel(first):
    def kernel(place, parts, stream, residual, gain, *rest):
        width = stream.shape[1]
        total = parts[0].astype(F32)
        for p in range(1, parts.shape[0]):
            total = total + parts[p].astype(F32)
        x = stream[...].astype(F32)
        rstd = lax.rsqrt(jnp.mean(x * x, 1, keepdims=True) + EPSILON)
        gain_out = rest[-1]
        gain_out[...] = jnp.broadcast_to(jnp.sum(total * x * rstd, 0, keepdims=True), gain_out.shape)
        weighted = total * gain[...]
        dot = jnp.sum(weighted * x, 1, keepdims=True)
        grad = rstd * weighted - x * (rstd * rstd * rstd * dot / width) + residual[:, :width].astype(F32)
        low = grad.astype(BF16)
        if first:
            rest[0][...] = low
        else:
            u, grad_out = rest[:2]
            grad_out[:, :width] = low
            grad_out[:, width:] = two_parts(jnp.sum(low.astype(F32) * u[...], 1, keepdims=True))

    return kernel


def shifted(shard, axis, by):
    peers = lax.axis_size(axis)
    pairs = [(i, i + by) for i in range(peers) if 0 <= i + by < peers]
    return lax.ppermute(shard, axis, pairs)


def gather_pieces(shard, axis):
    peers = lax.axis_size(axis)
    return [shard] + [
        lax.ppermute(shard, axis, [(i, i ^ s) for i in range(peers)]) for s in range(1, peers)
    ]


def padded(count, unit):
    return -(-count // unit) * unit


def swap(blocks, axis):
    return lax.all_to_all(blocks, axis, 0, 0)


def shards(
    hidden, cotangent, norm_gain, w_in_zx, w_in_dt, w_in_bc, conv_x, conv_x_bias, conv_bc,
    conv_bc_bias, dt_bias, a_log, d_skip, gate_norm, w_out,
):
    batch, length, width = hidden.shape
    rows = batch * length
    peers = lax.axis_size("head")
    ranks = lax.axis_size("seq")
    share = rows // peers
    layers, inner = w_out.shape[:2]
    heads = dt_bias.shape[1]
    head_size = inner // heads
    state = w_in_bc.shape[2] // 2
    inner_total = inner * peers
    dims = (batch, length, inner, heads, head_size, state)
    place = lax.axis_index("head").astype(jnp.int32).reshape(1)

    hidden_rows = hidden.reshape(rows, width)
    cot_rows = cotangent.reshape(rows, width)
    w_zx = jnp.transpose(w_in_zx, (0, 2, 1, 3))
    w_dt = jnp.pad(w_in_dt, ((0, 0), (0, 0), (0, LANES - heads)))
    head_par = jnp.pad(jnp.stack([dt_bias, a_log, d_skip], 1), ((0, 0), (0, 5), (0, LANES - heads)))
    taps_x = jnp.pad(jnp.concatenate([conv_x, conv_x_bias[:, None]], 1), ((0, 0), (0, 3), (0, 0)))
    taps_bc = jnp.pad(jnp.concatenate([conv_bc, conv_bc_bias[:, None]], 1), ((0, 0), (0, 3), (0, 0)))
    gates = gate_norm[:, None]
    gains = norm_gain[:, None]

    def norm_low(x, gain):
        x = x.astype(F32)
        return (x * lax.rsqrt(jnp.mean(x * x, -1, keepdims=True) + EPSILON) * gain).astype(BF16)

    wide = width + LANES
    take = lambda a: pl.BlockSpec((share, a.shape[1]), lambda _, at: (at[0], 0))
    hidden_halo = shifted(hidden[:, length - HALO :], "seq", 1)
    normed = norm_low(hidden_rows, norm_gain[0])
    halo = norm_low(hidden_halo, norm_gain[0]).reshape(batch * HALO, width)
    stream = hidden_rows
    saved = []
    for l in range(layers):
        last = l == layers - 1
        sub = lambda a, extra=None: layer_spec(a, l, extra)
        pad = batch * (length + 8)
        gate, padx, padbc, prex, prebc, step, cum, pay = call(
            forward_kernel(dims),
            [
                ((rows, inner), F32), ((pad, inner), F32), ((pad, 2 * state), F32),
                ((rows, inner), F32), ((rows, 2 * state), F32),
                ((rows, LANES), F32), ((rows, LANES), F32), ((state, batch * inner + LANES), BF16),
            ],
            [normed, halo, w_zx, w_zx, w_in_bc, w_dt, taps_x, taps_bc, head_par],
            [None, None, sub(w_zx, 0), sub(w_zx, 1), sub(w_in_bc), sub(w_dt), sub(taps_x), sub(taps_bc),
             sub(head_par)],
        )
        parts = swap(pay.reshape(ranks, state // ranks, batch * inner + LANES), "seq")
        local = call(
            local_kernel(dims),
            [((rows, inner), F32)],
            [prex, prebc, step, cum, head_par],
            [None] * 4 + [sub(head_par)],
            [pltpu.VMEM((length, inner), F32)],
        )[0]
        entered = call(
            scan_kernel(head_size, False),
            [((ranks, state // ranks, batch * inner), BF16)],
            [parts, parts],
        )[0]
        entered = swap(entered, "seq").reshape(state, batch * inner)
        kept = dict(
            normed=normed, stream=stream, gate=gate, padx=padx, padbc=padbc, prex=prex, prebc=prebc,
            step=step, cum=cum, parts=parts, entered=entered,
        )
        args = [local, gate, prebc, cum, entered, gates, w_out]
        specs = [None] * 5 + [sub(gates), sub(w_out)]
        outs = [((rows, inner), F32), ((rows, width if last else wide), BF16)]
        if last:
            args += [cot_rows]
            specs += [None]
            outs += [((8, length), F32)]
        mixed, branch, *sums = call(mix_kernel(dims, last), outs, args, specs)
        kept["mixed"] = mixed
        if last:
            kept["sources"] = gather_pieces(sums[0], "head")
        if last:
            branch_share = lax.psum_scatter(branch, "head", scatter_dimension=0, tiled=True)
        else:
            parts = swap(branch.reshape(peers, share, wide), "head")
            stream, low_share, kept["u"] = call(
                join_kernel(inner_total),
                [((share, width), F32), ((share, wide), BF16), ((share, width), F32)],
                [parts, stream, gains],
                [None, take(stream) if l == 0 else None, layer_spec(gains, l + 1)],
                prefetch=place,
            )
            normed = lax.all_gather(low_share, "head", axis=0, tiled=True)
            kept["sources"] = [normed]
            halo = shifted(normed.reshape(batch, length, wide)[:, length - HALO :], "seq", 1)
            halo = halo.reshape(batch * HALO, wide)
        saved.append(kept)

    grad = cot_rows
    residual = None
    done = [None] * layers
    gain_rows = [None] * layers
    after_sum = None
    head_rows = -(-heads // 8) * 8
    for l in range(layers - 1, -1, -1):
        last = l == layers - 1
        sub = lambda a, extra=None: layer_spec(a, l, extra)
        kept = saved[l]
        sources = kept["sources"]
        dmix, dgate, normed_out, pay, gn_grad, *rstd = call(
            gate_back_kernel(dims, inner_total, last, peers),
            [((rows, inner), F32), ((rows, inner), BF16), ((rows, inner), BF16),
             ((state, batch * inner), BF16), ((8, inner), F32)] + [((rows, LANES), F32)] * last,
            [grad, w_out, kept["mixed"], kept["gate"], kept["prebc"], kept["cum"], gates, *sources],
            [None, sub(w_out), None, None, None, None, sub(gates)] + [None] * len(sources),
        )
        back = swap(pay.reshape(ranks, state // ranks, batch * inner), "seq")
        dx_local, dbc_local, dcum_local = call(
            local_back_kernel(dims),
            [((rows, inner), F32), ((rows, 2 * state), F32), ((rows, LANES), F32)],
            [dmix, kept["prex"], kept["prebc"], kept["step"], kept["cum"]],
            scratch=[pltpu.VMEM((length, inner), F32)],
        )
        returned = call(
            scan_kernel(head_size, True),
            [((ranks, state // ranks, batch * inner), BF16)],
            [back, kept["parts"]],
        )[0]
        returned = swap(returned, "seq").reshape(state, batch * inner)
        zg, wo = call(
            early_weights_kernel,
            [((width + 16, inner), BF16), ((inner, width), BF16)],
            [kept["normed"], dgate, normed_out, grad, gn_grad],
        )
        if last:
            final_share = call(
                final_kernel,
                [((share, width), BF16)],
                [branch_share, kept["stream"], rstd[0]],
                [None, take(kept["stream"]) if l == 0 else None, take(rstd[0])],
                prefetch=place,
            )[0]
            returned, final_share = lax.optimization_barrier((returned, final_share))
            final_out = swap(jnp.broadcast_to(final_share[None], (peers,) + final_share.shape), "head")
        else:
            returned, zg, wo = lax.optimization_barrier((returned, zg, wo))
        gpx, gpbc, dstep, headx, headbc, tapx, tapbc, head_grads = call(
            scan_back_kernel(dims),
            [((rows, inner), F32), ((rows, 2 * state), F32), ((rows, LANES), BF16),
             ((batch * 8, inner), F32), ((batch * 8, 2 * state), F32),
             ((8, inner), F32), ((8, 2 * state), F32), ((8, LANES), F32)],
            [dmix, kept["prex"], kept["prebc"], kept["padx"], kept["padbc"], kept["step"], kept["cum"],
             kept["entered"], returned, head_par, dx_local, dbc_local, dcum_local],
            [None] * 9 + [sub(head_par)] + [None] * 3,
        )
        if last:
            dstep, final_out = lax.optimization_barrier((dstep, final_out))
        else:
            dstep, zg, wo, done[l + 1] = lax.optimization_barrier((dstep, zg, wo, done[l + 1]))
            zg, wo = lax.psum((zg, wo), "seq")
        aheadx = shifted(headx, "seq", -1)
        aheadbc = shifted(headbc, "seq", -1)
        grx, grbc, part = call(
            conv_back_kernel(dims),
            [((rows, inner), BF16), ((rows, 2 * state), BF16), ((rows, width), BF16)],
            [gpx, gpbc, aheadx, aheadbc, taps_x, taps_bc, dgate, dstep, w_zx, w_zx, w_in_bc, w_dt],
            [None] * 4 + [sub(taps_x), sub(taps_bc), None, None, sub(w_zx, 0), sub(w_zx, 1), sub(w_in_bc),
                          sub(w_dt)],
            [pltpu.VMEM((length + 8, inner), F32), pltpu.VMEM((length + 8, 2 * state), F32)],
        )
        parts = swap(part.reshape(peers, share, width), "head")
        zv_rows = padded(width + 16 + head_rows * (width // inner), 1 if l else 16 * ranks)
        bc_rows = padded((layers - l) * (width + 16), 1 if l else 16 * ranks)
        zv_shape, bc_shape = (zv_rows, inner), (bc_rows, 2 * state)
        args = [kept["normed"], grx, grbc, dstep, tapx, tapbc, head_grads]
        if last:
            zv, bc = call(late_weights_kernel(head_rows, width, False), [(zv_shape, BF16), (bc_shape, BF16)], args)
        else:
            lanes = math.gcd(inner, 2 * state)
            zv_block, bc_block = zv_rows * inner // ranks // lanes, bc_rows * 2 * state // ranks // lanes
            pack = call(
                late_weights_kernel(head_rows, width, True),
                [((ranks, zv_block + bc_block, lanes), BF16)],
                args + [bc],
                scratch=[pltpu.VMEM(zv_shape, BF16), pltpu.VMEM(bc_shape, BF16)],
            )[0]
        if last:
            parts, zv, zg, wo = lax.optimization_barrier((parts, zv, zg, wo))
            zg, wo, zv = lax.psum((zg, wo, zv), "seq")
        else:
            parts, pack = lax.optimization_barrier((parts, pack))
        outs = [((share, width if l == 0 else wide), BF16), ((8, width), F32)]
        args = [parts, kept["stream"], grad if last else residual, gains]
        specs = [None, take(kept["stream"]) if l == 0 else None, take(grad) if last else None, sub(gains)]
        if l > 0:
            args += [saved[l - 1]["u"]]
            specs += [None]
        residual, gain_grad = call(norm_back_kernel(l == 0), outs, args, specs, prefetch=place)
        if not last:
            residual, pack = lax.optimization_barrier((residual, pack))
            pack = swap(pack, "seq")
        grad = lax.all_gather(residual, "head", axis=0, tiled=True)
        if not last:
            grad, pack = lax.optimization_barrier((grad, pack))
            pack = jnp.sum(pack.astype(F32), 0)
        gain_rows[l] = gain_grad[0]
        done[l] = (zg, wo, zv if last else None)
    gain = jnp.stack(gain_rows).reshape(-1, lanes)
    gain_count = gain.shape[0]
    gain = jnp.pad(gain, ((0, padded(gain_count, 16) - gain_count), (0, 0)))
    low = jnp.concatenate([pack[zv_block:], gain], 0).astype(BF16)
    low = sum(p.astype(F32) for p in gather_pieces(low, "head"))
    low = jnp.concatenate([pack[:zv_block], low], 0).astype(BF16)
    low, zg, wo = lax.optimization_barrier((low, zg, wo))
    done[0] = (zg, wo, None)
    low = swap(jnp.broadcast_to(low[None], (ranks,) + low.shape), "seq")

    def unpacked(part, columns):
        part = part.reshape(ranks, columns // lanes, -1, lanes)
        return jnp.moveaxis(part, 1, 2).reshape(-1, columns)

    zv = unpacked(low[:, :zv_block], inner)[: width + 16 + head_rows * (width // inner)]
    bc = unpacked(low[:, zv_block : zv_block + bc_block], 2 * state)[: layers * (width + 16)]
    gain_sum = low[:, zv_block + bc_block : zv_block + bc_block + gain_count].astype(F32)
    gain_sum = jnp.sum(gain_sum, 0).reshape(layers, width)
    done[0] = (*done[0][:2], zv)
    zg, wo, zv = [jnp.stack(d) for d in zip(*done)]
    bc = bc.reshape(layers, width + 16, 2 * state)
    small = zv[:, width:].astype(F32)
    steps = small[:, 16:].reshape(layers, width // inner, head_rows, inner)[:, :, :heads]
    steps = jnp.moveaxis(steps, 2, 3).reshape(layers, width, heads)
    return (
        final_out.astype(F32).reshape(hidden.shape),
        grad.astype(F32).reshape(hidden.shape),
        gain_sum,
        jnp.stack([zg[:, :width], zv[:, :width]], 2).astype(F32),
        steps,
        bc[:, :width].astype(F32),
        small[:, :4],
        small[:, 4],
        bc[:, width : width + 4].astype(F32),
        bc[:, width + 4].astype(F32),
        small[:, 8, :heads],
        small[:, 9, :heads],
        small[:, 10, :heads],
        zg[:, width].astype(F32),
        wo.astype(F32),
    )


def solution(mesh):
    tokens = P(None, "seq", None)
    heads = P(None, "head")
    last = P(None, None, "head")
    placed = (
        tokens, tokens, P(), P(None, None, None, "head"), last, P(), last, heads, P(), P(), heads, heads,
        heads, heads, P(None, "head", None),
    )
    results = (
        tokens, tokens, P(), P(None, None, None, "head"), last, P(), last, heads, P(), P(), heads, heads,
        heads, heads, P(None, "head", None),
    )
    return jax.shard_map(shards, mesh=mesh, in_specs=placed, out_specs=results, check_vma=False)
```
